32 devices in a mesh: head: 4 (over y, x), pb: 8 (over z, core).
Axes of the slice: x: 2, y: 2, z: 4, core: 2. Of those that a mesh axis runs over, the one named last changes fastest.
Arguments:
- pair: bfloat16 [512, 512, 128], P('pb', 'head'), may hold values from -6 to 6
- tokens: bfloat16 [512, 768], P('pb'), may hold values from -6 to 6
- token_mask: int32 [512], replicated, may hold values from 0 to 1, as said below
- w_gu: bfloat16 [2, 128, 512], replicated, may hold values from -0.5 to 0.5
- w_down: bfloat16 [2, 256, 128], replicated, may hold values from -0.375 to 0.375
- w_bias: bfloat16 [128, 32], replicated, may hold values from -0.5 to 0.5
- w_q: bfloat16 [2, 768, 768], P(None, None, 'head'), may hold values from -0.21875 to 0.21875
- w_k: bfloat16 [2, 768, 768], P(None, None, 'head'), may hold values from -0.21875 to 0.21875
- w_v: bfloat16 [2, 768, 768], P(None, None, 'head'), may hold values from -0.21875 to 0.21875
- w_gate: bfloat16 [2, 768, 768], P(None, None, 'head'), may hold values from -0.21875 to 0.21875
- w_out: bfloat16 [2, 768, 768], P(None, 'head'), may hold values from -0.875 to 0.875
Outputs:
- updated: bfloat16 [512, 768], P('pb')
The draws below stay inside these ranges and needn't reach their ends.
Inputs may be any that keep to these rules, and one draw needn't show every extreme that they name: `token_mask`: ones on a prefix of the tokens and zeros after it; at least 128 ones and at least one zero.
All inputs are finite; a program needn't handle non-finite values.
Results may differ from the reference program's by a relative error of at most 0.019.
Values may be sent and summed in bfloat16 or wider, within the bound.
A program may use at most 64 MiB of HBM per device.

```python
import jax
import jax.numpy as jnp
from jax import lax

C = 128
FFP = 256
D = 768
H = 16
TRANS = 2
LAYERS = 2
HD = 48
N = 512


def draw_token_mask(key, part):
    real_count = jax.random.randint(jax.random.fold_in(key, 17), (), N // 4, N)
    return (jnp.arange(N) < real_count).astype(jnp.int32)


def draw_tokens(key, part):
    scale_key = jax.random.fold_in(key, 31)
    value_key = jax.random.fold_in(key, 37)
    log_scale = jax.random.uniform(scale_key, (N, 1), jnp.float32, -3.0, 0.4)
    row_scale = jnp.exp(log_scale)
    raw = jax.random.truncated_normal(value_key, -4.0, 4.0, (N, D), jnp.float32)
    return (raw * row_scale).astype(jnp.bfloat16)


def level_of(rng, dims, pieces, smallest, largest):
    loudness = 1.0
    for position, blocks in pieces:
        draws = jax.random.uniform(jax.random.fold_in(jax.random.fold_in(rng, 6), position), (blocks,), jnp.float32, smallest / len(pieces), largest / len(pieces))
        loudness = loudness * jnp.repeat(jnp.exp(draws), dims[position] // blocks).reshape((-1,) + (1,) * (len(dims) - 1 - position))
    return loudness


def noise(rng, shape, scale, most, pieces=(), kind=jnp.bfloat16):
    factor_of = level_of(rng, shape, pieces, -0.22, 0.18) if pieces else 1.0
    result = jax.random.normal(rng, shape, jnp.float32) * scale * factor_of
    return jnp.minimum(jnp.maximum(result, -most), most).astype(kind)


def setup_inputs(seed: int = 0) -> dict:
    streams_of = jax.random.split(jax.random.key(seed), 12)
    return {
        "pair": noise(streams_of[0], (N, N, C), 1.0, 6.0, ((0, 8), (1, 4))),
        "tokens": draw_tokens(jax.random.fold_in(streams_of[11], 71), 0),
        "token_mask": draw_token_mask(jax.random.fold_in(streams_of[11], 71), 0),
        "w_gu": noise(streams_of[3], (TRANS, C, 2 * FFP), C ** -0.5, 0.5),
        "w_down": noise(streams_of[4], (TRANS, FFP, C), FFP ** -0.5, 0.375),
        "w_bias": noise(streams_of[5], (C, LAYERS * H), C ** -0.5, 0.5),
        "w_q": noise(streams_of[6], (LAYERS, D, D), D ** -0.5, 0.21875, ((2, 4),)),
        "w_k": noise(streams_of[7], (LAYERS, D, D), D ** -0.5, 0.21875, ((2, 4),)),
        "w_v": noise(streams_of[8], (LAYERS, D, D), D ** -0.5, 0.21875, ((2, 4),)),
        "w_gate": noise(streams_of[9], (LAYERS, D, D), D ** -0.5, 0.21875, ((2, 4),)),
        "w_out": noise(streams_of[10], (LAYERS, D, D), (D // 16) ** -0.5, 0.875, ((1, 4),)),
    }


def normalize(values):
    values = values.astype(jnp.float32)
    center = values - lax.optimization_barrier(jnp.mean(values, axis=-1, keepdims=True))
    spread = lax.optimization_barrier(jnp.mean(center * center, axis=-1, keepdims=True))
    return center * lax.rsqrt(spread + 1e-05)

def transition(pair_rows, w_updown, w_back):
    normed = normalize(pair_rows).astype(jnp.bfloat16)
    mixed = jnp.dot(normed, w_updown, preferred_element_type=jnp.float32)
    hidden = (jax.nn.silu(mixed[:, :FFP]) * mixed[:, FFP:]).astype(jnp.bfloat16)
    summed = pair_rows.astype(jnp.float32) + jnp.dot(hidden, w_back, preferred_element_type=jnp.float32)
    return summed.astype(jnp.bfloat16)

def reference(pair, tokens, token_mask, w_gu, w_down, w_bias, w_q, w_k, w_v, w_gate, w_out):

    def one_row(pair_row):
        current = pair_row
        for section_index in range(TRANS):
            current = transition(current, w_gu[section_index], w_down[section_index])
        normed = normalize(current).astype(jnp.bfloat16)
        return jnp.dot(normed, w_bias, preferred_element_type=jnp.float32).astype(jnp.bfloat16)
    bias_all = lax.map(one_row, pair).reshape(N, N, LAYERS, H)
    is_real = token_mask == 1
    real_rows = is_real.astype(jnp.float32)
    state = tokens.astype(jnp.float32)
    for layer_index in range(LAYERS):
        normed = normalize(state).astype(jnp.bfloat16)
        queries = jnp.dot(normed, w_q[layer_index], preferred_element_type=jnp.float32).astype(jnp.bfloat16)
        key_proj = jnp.dot(normed, w_k[layer_index], preferred_element_type=jnp.float32).astype(jnp.bfloat16)
        value_proj = jnp.dot(normed, w_v[layer_index], preferred_element_type=jnp.float32).astype(jnp.bfloat16)
        gate_vals = jnp.dot(normed, w_gate[layer_index], preferred_element_type=jnp.float32).astype(jnp.bfloat16)
        query_heads = queries.astype(jnp.float32).reshape(N, H, HD)
        key_heads = key_proj.astype(jnp.float32).reshape(N, H, HD)
        value_heads = value_proj.astype(jnp.float32).reshape(N, H, HD)
        scores = jnp.einsum('ihd,jhd->hij', query_heads, key_heads) * (1.0 / HD ** 0.5)
        scores = scores + jnp.transpose(bias_all[:, :, layer_index, :], (2, 0, 1)).astype(jnp.float32)
        scores = jnp.where(is_real[None, None, :], scores, -1e+30)
        weights = jax.nn.softmax(scores, axis=-1)
        attended = jnp.einsum('hij,jhd->ihd', weights, value_heads).reshape(N, D)
        gated = (attended * jax.nn.sigmoid(gate_vals.astype(jnp.float32))).astype(jnp.bfloat16)
        update = jnp.dot(gated, w_out[layer_index], preferred_element_type=jnp.float32)
        state = state + real_rows[:, None] * update
    return state.astype(jnp.bfloat16)
```

```python
import functools

import jax
import jax.numpy as jnp
from jax import lax
from jax.experimental import pallas as pl
from jax.experimental.pallas import tpu as pltpu
from jax.sharding import PartitionSpec as P

TRANS = 2
LAYERS = 2
HD = 48
CORES = 2
STEP_ROWS = 16
LANES = 128
F32 = jnp.float32
BF16 = jnp.bfloat16


def normalize(values):
    inverse = 1.0 / values.shape[-1]
    center = values - jnp.sum(values, axis=-1, keepdims=True) * inverse
    spread = jnp.sum(center * center, axis=-1, keepdims=True) * inverse
    return center * lax.rsqrt(spread + 1e-05)


def matmul(left, right):
    return jnp.dot(left, right, preferred_element_type=F32)


def matmul_t(left, right):
    return lax.dot_general(left, right, (((1,), (1,)), ((), ())), preferred_element_type=F32)


def step_kernel(
    head_count,
    pb_count,
    pair_hbm,
    tokens_ref,
    mask_ref,
    gu_ref,
    down_ref,
    bias_w_ref,
    q_hbm,
    k_hbm,
    v_hbm,
    gate_hbm,
    out_hbm,
    result_ref,
    pair_v,
    gu_v,
    wq_v,
    wk_v,
    wv_v,
    wg_v,
    wo_v,
    bias_out,
    bias_in,
    kv_all,
    q_v,
    gate_v,
    sums_out,
    sums_in,
    rows_all,
    pair_sem,
    weight_sem,
    bias_send,
    bias_recv,
    kv_send,
    kv_recv,
    fwd_send,
    fwd_recv,
    sums_send,
    sums_recv,
    rows_send,
    rows_recv,
):
    rows, cols, channels = pair_hbm.shape
    width = q_hbm.shape[2]
    features = tokens_ref.shape[1]
    local_heads = width // HD
    heads_all = local_heads * head_count
    own_rows = rows // head_count
    chips = pb_count // CORES
    col_blocks = cols // LANES
    steps = (rows // STEP_ROWS) * col_blocks
    hidden = down_ref.shape[1]

    head = lax.axis_index("head")
    pb = lax.axis_index("pb")
    core = lax.rem(pb, CORES)
    chip = pb // CORES
    partner = chip * CORES + (1 - core)

    def head_peer(k):
        return lax.rem(head + k, head_count)

    def chip_peer(d):
        return lax.rem(chip + d, chips) * CORES + core

    def chip_source(d):
        return lax.rem(chip + chips - d, chips) * CORES + core

    weight_copies = []
    for index, (source, target) in enumerate(
        ((k_hbm, wk_v), (v_hbm, wv_v), (q_hbm, wq_v), (gate_hbm, wg_v), (out_hbm, wo_v))
    ):
        copy = pltpu.make_async_copy(source, target, weight_sem.at[index])
        copy.start()
        weight_copies.append(copy)

    def pair_copy(n):
        where = (
            pl.ds((n // col_blocks) * STEP_ROWS, STEP_ROWS),
            pl.ds(pl.multiple_of((n % col_blocks) * LANES, LANES), LANES),
        )
        return pltpu.make_async_copy(
            pair_hbm.at[where[0], where[1], :], pair_v.at[where[0], where[1], :], pair_sem.at[n]
        )

    for n in range(steps):
        pair_copy(n).start()

    barrier = pltpu.get_barrier_semaphore()
    for k in range(1, head_count):
        pl.semaphore_signal(
            barrier, inc=1, device_id=(head_peer(k), pb), device_id_type=pl.DeviceIdType.MESH
        )
    for d in range(1, chips):
        pl.semaphore_signal(
            barrier, inc=1, device_id=(head, chip_peer(d)), device_id_type=pl.DeviceIdType.MESH
        )
    pl.semaphore_signal(
        barrier, inc=1, device_id=(head, partner), device_id_type=pl.DeviceIdType.MESH
    )
    pl.semaphore_wait(barrier, head_count + chips - 1)

    def remote(source, target, send, recv, where):
        return pltpu.make_async_remote_copy(
            src_ref=source,
            dst_ref=target,
            send_sem=send,
            recv_sem=recv,
            device_id=where,
            device_id_type=pl.DeviceIdType.MESH,
        )

    def kv_copy(layer, d):
        block = kv_all.at[layer, pb]
        return remote(
            block, block, kv_send.at[layer, d], kv_recv.at[layer, d], (head, chip_peer(d))
        )

    def kv_forward(layer, d):
        block = kv_all.at[layer, chip_source(d)]
        return remote(block, block, fwd_send.at[layer, d], fwd_recv.at[layer, d], (head, partner))

    def project(layer, normed):
        keys = matmul(normed, wk_v[layer]).astype(BF16)
        values = matmul(normed, wv_v[layer]).astype(BF16)
        kv_all[layer, pb] = jnp.concatenate([keys, values], axis=1)
        for d in range(1, chips):
            kv_copy(layer, d).start()
        kv_forward(layer, 0).start()
        q_v[...] = matmul(normed, wq_v[layer]).astype(BF16)
        gate_v[...] = matmul(normed, wg_v[layer]).astype(BF16)

    def forward_kv(layer):
        for d in range(1, chips):
            kv_copy(layer, d).wait_recv()
            kv_forward(layer, d).start()

    def finish_kv(layer):
        for d in range(chips):
            kv_forward(layer, d).wait_recv()

    for copy in weight_copies[:4]:
        copy.wait()
    project(0, normalize(tokens_ref[...].astype(F32)).astype(BF16))

    for section in range(TRANS):
        gu_v[section, :, :hidden] = (gu_ref[section, :, :hidden].astype(F32) * 0.5).astype(BF16)
        gu_v[section, :, hidden:] = gu_ref[section, :, hidden:]
    bias_w = jnp.transpose(bias_w_ref[...].astype(F32)).astype(BF16)

    def bias_copy(n, k):
        where = (
            pl.ds((n // col_blocks) * STEP_ROWS, STEP_ROWS),
            pl.ds(pl.multiple_of((n % col_blocks) * LANES, LANES), LANES),
        )
        return remote(
            bias_out.at[head_peer(k), :, :, where[0], where[1]],
            bias_in.at[head, :, :, where[0], where[1]],
            bias_send.at[n, k],
            bias_recv.at[n, k],
            (head_peer(k), pb),
        )

    half = STEP_ROWS // 2

    def pair_step(n, carry):
        pair_copy(n).wait()
        first_row = (n // col_blocks) * STEP_ROWS
        first_col = pl.multiple_of((n % col_blocks) * LANES, LANES)

        @pl.when(n == steps - 1)
        def _():
            forward_kv(0)

        planes = []
        for part in range(2):
            current = pair_v[
                pl.ds(first_row + part * half, half), pl.ds(first_col, LANES), :
            ].reshape(half * LANES, channels)
            for section in range(TRANS):
                wide = current.astype(F32)
                normed = normalize(wide).astype(BF16)
                mixed = matmul(normed, gu_v[section])
                gate = mixed[:, :hidden]
                units = ((gate + gate * jnp.tanh(gate)) * mixed[:, hidden:]).astype(BF16)
                current = (wide + matmul(units, down_ref[section])).astype(BF16)
            normed = normalize(current.astype(F32)).astype(BF16)
            projected = matmul_t(bias_w, normed)
            planes += [projected[:, i * LANES : (i + 1) * LANES] for i in range(half)]
        by_head = jnp.transpose(jnp.stack(planes, axis=0), (1, 0, 2)).astype(BF16)
        for layer in range(LAYERS):
            for target in range(head_count):
                start = layer * heads_all + target * local_heads
                bias_out[target, layer, :, pl.ds(first_row, STEP_ROWS), pl.ds(first_col, LANES)] = (
                    by_head[start : start + local_heads]
                )
        bias_in[head, :, :, pl.ds(first_row, STEP_ROWS), pl.ds(first_col, LANES)] = bias_out[
            head, :, :, pl.ds(first_row, STEP_ROWS), pl.ds(first_col, LANES)
        ]
        for k in range(1, head_count):
            bias_copy(n, k).start()
        return carry

    lax.fori_loop(0, steps, pair_step, 0)

    mask_row = mask_ref[...]
    real_count = jnp.sum(mask_row.astype(F32), axis=1, keepdims=True)
    is_real = mask_row == 1
    own_first = pb * rows + head * own_rows
    row_index = (lax.broadcasted_iota(jnp.int32, (own_rows, 1), 0) + own_first).astype(F32)
    row_real = (row_index < real_count).astype(F32)
    state = tokens_ref[pl.ds(head * own_rows, own_rows), :].astype(F32)
    lane = lax.broadcasted_iota(jnp.int32, (rows, 2 * width), 1)
    scale = 1.0 / HD**0.5

    def bias_wait(n, carry):
        for k in range(1, head_count):
            bias_copy(n, k).wait_recv()
        return carry

    def sums_copy(layer, k):
        return remote(
            sums_out.at[layer, head_peer(k)],
            sums_in.at[layer, k],
            sums_send.at[layer, k],
            sums_recv.at[layer, k],
            (head_peer(k), pb),
        )

    def rows_copy(layer, k):
        block = rows_all.at[layer, head]
        return remote(
            block, block, rows_send.at[layer, k], rows_recv.at[layer, k], (head_peer(k), pb)
        )

    for layer in range(LAYERS):
        if layer:
            forward_kv(layer)
        finish_kv(layer)
        if not layer:
            lax.fori_loop(0, steps, bias_wait, 0)
            weight_copies[4].wait()
        keys_values = kv_all[layer].reshape(pb_count * rows, 2 * width)
        queries = jnp.concatenate([q_v[...], jnp.zeros((rows, width), BF16)], axis=1)
        spread_q = jnp.concatenate(
            [
                jnp.where((lane >= h * HD) & (lane < (h + 1) * HD), queries, jnp.zeros_like(queries))
                for h in range(local_heads)
            ],
            axis=0,
        )
        bias = jnp.concatenate(
            [
                bias_in[source, layer].reshape(local_heads * rows, cols)
                for source in range(head_count)
            ],
            axis=1,
        )
        scores = matmul_t(spread_q, keys_values) * scale + bias.astype(F32)
        scores = jnp.where(is_real, scores, -1e30)
        peak = jnp.max(scores, axis=1, keepdims=True)
        weights = jnp.exp(scores - peak)
        total = jnp.sum(weights, axis=1, keepdims=True)
        mixed = matmul(weights.astype(BF16), keys_values) / total
        attended = jnp.zeros((rows, 2 * width), F32)
        for h in range(local_heads):
            keep = (lane >= width + h * HD) & (lane < width + (h + 1) * HD)
            attended = attended + jnp.where(keep, mixed[h * rows : (h + 1) * rows], 0.0)
        gated = (attended[:, width:] * jax.nn.sigmoid(gate_v[...].astype(F32))).astype(BF16)
        partial = matmul(gated, wo_v[layer])
        sums_out[layer] = partial.astype(BF16).reshape(head_count, own_rows, features)
        for k in range(1, head_count):
            sums_copy(layer, k).start()
        update = sums_out[layer, head].astype(F32)
        for k in range(1, head_count):
            sums_copy(layer, k).wait_recv()
            update = update + sums_in[layer, k].astype(F32)
        state = state + row_real * update
        last = layer == LAYERS - 1
        rows_all[layer, head] = (state if last else normalize(state)).astype(BF16)
        for k in range(1, head_count):
            rows_copy(layer, k).start()
        for k in range(1, head_count):
            rows_copy(layer, k).wait_recv()
        gathered = rows_all[layer].reshape(rows, features)
        if last:
            result_ref[...] = gathered
        else:
            project(layer + 1, gathered)

    def bias_sent(n, carry):
        for k in range(1, head_count):
            bias_copy(n, k).wait_send()
        return carry

    lax.fori_loop(0, steps, bias_sent, 0)
    for layer in range(LAYERS):
        for d in range(1, chips):
            kv_copy(layer, d).wait_send()
        for d in range(chips):
            kv_forward(layer, d).wait_send()
        for k in range(1, head_count):
            sums_copy(layer, k).wait_send()
            rows_copy(layer, k).wait_send()


def on_device(
    head_count, pb_count, pair, tokens, token_mask, w_gu, w_down, w_bias, w_q, w_k, w_v, w_gate, w_out
):
    rows, cols, channels = pair.shape
    width = w_q.shape[2]
    features = tokens.shape[1]
    local_heads = width // HD
    own_rows = rows // head_count
    chips = pb_count // CORES
    steps = (rows // STEP_ROWS) * (cols // LANES)
    vmem = pl.BlockSpec(memory_space=pltpu.VMEM)
    anywhere = pl.BlockSpec(memory_space=pl.ANY)
    dma = pltpu.SemaphoreType.DMA
    bias_shape = (head_count, LAYERS, local_heads, rows, cols)
    return pl.pallas_call(
        functools.partial(step_kernel, head_count, pb_count),
        out_shape=jax.ShapeDtypeStruct((rows, features), BF16),
        in_specs=[anywhere] + [vmem] * 5 + [anywhere] * 5,
        out_specs=vmem,
        scratch_shapes=[
            pltpu.VMEM(pair.shape, BF16),
            pltpu.VMEM(w_gu.shape, BF16),
            pltpu.VMEM(w_q.shape, BF16),
            pltpu.VMEM(w_k.shape, BF16),
            pltpu.VMEM(w_v.shape, BF16),
            pltpu.VMEM(w_gate.shape, BF16),
            pltpu.VMEM(w_out.shape, BF16),
            pltpu.VMEM(bias_shape, BF16),
            pltpu.VMEM(bias_shape, BF16),
            pltpu.VMEM((LAYERS, pb_count, rows, 2 * width), BF16),
            pltpu.VMEM((rows, width), BF16),
            pltpu.VMEM((rows, width), BF16),
            pltpu.VMEM((LAYERS, head_count, own_rows, features), BF16),
            pltpu.VMEM((LAYERS, head_count, own_rows, features), BF16),
            pltpu.VMEM((LAYERS, head_count, own_rows, features), BF16),
            dma((steps,)),
            dma((5,)),
            dma((steps, head_count)),
            dma((steps, head_count)),
            dma((LAYERS, chips)),
            dma((LAYERS, chips)),
            dma((LAYERS, chips)),
            dma((LAYERS, chips)),
            dma((LAYERS, head_count)),
            dma((LAYERS, head_count)),
            dma((LAYERS, head_count)),
            dma((LAYERS, head_count)),
        ],
        compiler_params=pltpu.CompilerParams(
            collective_id=0, has_side_effects=True, vmem_limit_bytes=60 * 1024 * 1024
        ),
        name="diffusion_step",
    )(
        pair,
        tokens,
        token_mask.reshape(1, -1),
        w_gu,
        w_down,
        w_bias,
        w_q,
        w_k,
        w_v,
        w_gate,
        w_out,
    )


def solution(mesh):
    placed = (
        P("pb", "head", None),
        P("pb", None),
        P(),
        P(),
        P(),
        P(),
        P(None, None, "head"),
        P(None, None, "head"),
        P(None, None, "head"),
        P(None, None, "head"),
        P(None, "head", None),
    )
    return jax.shard_map(
        functools.partial(on_device, mesh.shape["head"], mesh.shape["pb"]),
        mesh=mesh,
        in_specs=placed,
        out_specs=P("pb", None),
        check_vma=False,
    )
```

```python
import functools

import jax
import jax.numpy as jnp
from jax import lax
from jax.experimental import pallas as pl
from jax.experimental.pallas import tpu as pltpu
from jax.sharding import PartitionSpec as P

TRANS = 2
LAYERS = 2
HD = 48
CORES = 2
STEP_ROWS = 16
LANES = 128
F32 = jnp.float32
BF16 = jnp.bfloat16


def normalize(values):
    inverse = 1.0 / values.shape[-1]
    center = values - jnp.sum(values, axis=-1, keepdims=True) * inverse
    spread = jnp.sum(center * center, axis=-1, keepdims=True) * inverse
    return center * lax.rsqrt(spread + 1e-05)


def matmul(left, right):
    return jnp.dot(left, right, preferred_element_type=F32)


def matmul_t(left, right):
    return lax.dot_general(left, right, (((1,), (1,)), ((), ())), preferred_element_type=F32)


def step_kernel(
    head_count,
    pb_count,
    pair_hbm,
    tokens_ref,
    mask_ref,
    gu_ref,
    down_ref,
    bias_w_ref,
    q_hbm,
    k_hbm,
    v_hbm,
    gate_hbm,
    out_hbm,
    result_ref,
    pair_v,
    gu_v,
    wide_w,
    out_w,
    bias_out,
    bias_in,
    kv_all,
    query_gate,
    gated_all,
    pair_sem,
    weight_sem,
    bias_send,
    bias_recv,
    kv_send,
    kv_recv,
    fwd_send,
    fwd_recv,
    gated_send,
    gated_recv,
    out_send,
    out_recv,
    out_fwd_send,
    out_fwd_recv,
):
    rows, cols, channels = pair_hbm.shape
    width = q_hbm.shape[1]
    features = tokens_ref.shape[1]
    local_heads = width // HD
    heads_all = local_heads * head_count
    half_width = width // CORES
    chips = pb_count // CORES
    col_blocks = cols // LANES
    steps = (rows // STEP_ROWS) * col_blocks
    hidden = down_ref.shape[1]

    head = lax.axis_index("head")
    pb = lax.axis_index("pb")
    core = lax.rem(pb, CORES)
    chip = pb // CORES
    partner = chip * CORES + (1 - core)

    def head_peer(k):
        return lax.rem(head + k, head_count)

    def chip_peer(d):
        return lax.rem(chip + d, chips) * CORES + core

    def chip_source(d):
        return lax.rem(chip + chips - d, chips) * CORES + core

    def weight_copies(layer):
        copies = [
            pltpu.make_async_copy(
                source.at[layer],
                wide_w.at[layer, index * width : (index + 1) * width],
                weight_sem.at[layer, index],
            )
            for index, source in enumerate((k_hbm, v_hbm, q_hbm, gate_hbm))
        ]
        for part in range(CORES):
            copies.append(
                pltpu.make_async_copy(
                    out_hbm.at[layer, part * half_width : (part + 1) * half_width],
                    out_w.at[layer, head, part],
                    weight_sem.at[layer, 4 + part],
                )
            )
        return copies

    def pair_copy(n):
        where = (
            pl.ds((n // col_blocks) * STEP_ROWS, STEP_ROWS),
            pl.ds(pl.multiple_of((n % col_blocks) * LANES, LANES), LANES),
        )
        return pltpu.make_async_copy(
            pair_hbm.at[where[0], where[1], :], pair_v.at[where[0], where[1], :], pair_sem.at[n]
        )

    for copy in weight_copies(0)[:4]:
        copy.start()
    for n in range(steps):
        pair_copy(n).start()
    for copy in weight_copies(0)[4:] + weight_copies(1):
        copy.start()

    barrier = pltpu.get_barrier_semaphore()
    for k in range(1, head_count):
        pl.semaphore_signal(
            barrier, inc=1, device_id=(head_peer(k), pb), device_id_type=pl.DeviceIdType.MESH
        )
    for d in range(1, chips):
        pl.semaphore_signal(
            barrier, inc=1, device_id=(head, chip_peer(d)), device_id_type=pl.DeviceIdType.MESH
        )
    pl.semaphore_signal(
        barrier, inc=1, device_id=(head, partner), device_id_type=pl.DeviceIdType.MESH
    )

    def remote(source, target, send, recv, where):
        return pltpu.make_async_remote_copy(
            src_ref=source,
            dst_ref=target,
            send_sem=send,
            recv_sem=recv,
            device_id=where,
            device_id_type=pl.DeviceIdType.MESH,
        )

    def kv_copy(layer, d):
        block = kv_all.at[layer, pb]
        return remote(
            block, block, kv_send.at[layer, d], kv_recv.at[layer, d], (head, chip_peer(d))
        )

    def kv_forward(layer, d):
        block = kv_all.at[layer, chip_source(d)]
        return remote(block, block, fwd_send.at[layer, d], fwd_recv.at[layer, d], (head, partner))

    def out_copy(layer, k):
        return remote(
            out_hbm.at[layer, pl.ds(pl.multiple_of(core * half_width, half_width), half_width)],
            out_w.at[layer, head, core],
            out_send.at[layer, k],
            out_recv.at[layer, k],
            (head_peer(k), pb),
        )

    def out_forward(layer, k):
        block = out_w.at[layer, lax.rem(head + head_count - k, head_count), core]
        return remote(
            block, block, out_fwd_send.at[layer, k], out_fwd_recv.at[layer, k], (head, partner)
        )

    def forward_out():
        for layer in range(LAYERS):
            for k in range(1, head_count):
                out_copy(layer, k).wait_recv()
                out_forward(layer, k).start()

    def gated_copy(layer, k):
        block = gated_all.at[layer, head]
        return remote(
            block, block, gated_send.at[layer, k], gated_recv.at[layer, k], (head_peer(k), pb)
        )

    def project(layer, normed):
        kv_all[layer, pb] = matmul_t(normed, wide_w[layer, : 2 * width]).astype(BF16)
        if not layer:
            pl.semaphore_wait(barrier, head_count + chips - 1)
        for d in range(1, chips):
            kv_copy(layer, d).start()
        kv_forward(layer, 0).start()
        if not layer:
            for which in range(LAYERS):
                for k in range(1, head_count):
                    out_copy(which, k).start()
        query_gate[...] = matmul_t(normed, wide_w[layer, 2 * width :]).astype(BF16)

    def forward_kv(layer):
        for d in range(1, chips):
            kv_copy(layer, d).wait_recv()
            kv_forward(layer, d).start()

    def finish_kv(layer):
        for d in range(chips):
            kv_forward(layer, d).wait_recv()

    for copy in weight_copies(0)[:4]:
        copy.wait()
    project(0, normalize(tokens_ref[...].astype(F32)).astype(BF16))

    for section in range(TRANS):
        gu_v[section, :, :hidden] = (gu_ref[section, :, :hidden].astype(F32) * 0.5).astype(BF16)
        gu_v[section, :, hidden:] = gu_ref[section, :, hidden:]
    bias_w = bias_w_ref[...]

    def bias_copy(n, k):
        where = (
            pl.ds((n // col_blocks) * STEP_ROWS, STEP_ROWS),
            pl.ds(pl.multiple_of((n % col_blocks) * LANES, LANES), LANES),
        )
        return remote(
            bias_out.at[head_peer(k), :, :, where[0], where[1]],
            bias_in.at[head, :, :, where[0], where[1]],
            bias_send.at[n, k],
            bias_recv.at[n, k],
            (head_peer(k), pb),
        )

    half = STEP_ROWS // 2

    def pair_step(n, carry):
        pair_copy(n).wait()
        first_row = (n // col_blocks) * STEP_ROWS
        first_col = pl.multiple_of((n % col_blocks) * LANES, LANES)

        @pl.when(n == steps - 1)
        def _():
            forward_kv(0)
            forward_out()

        planes = []
        for part in range(2):
            current = pair_v[
                pl.ds(first_row + part * half, half), pl.ds(first_col, LANES), :
            ].reshape(half * LANES, channels)
            for section in range(TRANS):
                wide = current.astype(F32)
                normed = normalize(wide).astype(BF16)
                mixed = matmul(normed, gu_v[section])
                gate = mixed[:, :hidden]
                units = ((gate + gate * jnp.tanh(gate)) * mixed[:, hidden:]).astype(BF16)
                current = (wide + matmul(units, down_ref[section])).astype(BF16)
            normed = normalize(current.astype(F32)).astype(BF16)
            projected = matmul_t(bias_w, normed)
            planes += [projected[:, i * LANES : (i + 1) * LANES] for i in range(half)]
        by_head = jnp.transpose(jnp.stack(planes, axis=0), (1, 0, 2)).astype(BF16)
        for layer in range(LAYERS):
            for target in range(head_count):
                start = layer * heads_all + target * local_heads
                bias_out[target, layer, :, pl.ds(first_row, STEP_ROWS), pl.ds(first_col, LANES)] = (
                    by_head[start : start + local_heads]
                )
        bias_in[head, :, :, pl.ds(first_row, STEP_ROWS), pl.ds(first_col, LANES)] = bias_out[
            head, :, :, pl.ds(first_row, STEP_ROWS), pl.ds(first_col, LANES)
        ]
        for k in range(1, head_count):
            bias_copy(n, k).start()
        return carry

    lax.fori_loop(0, steps, pair_step, 0)

    mask_row = mask_ref[...]
    real_count = jnp.sum(mask_row.astype(F32), axis=1, keepdims=True)
    is_real = mask_row == 1
    row_index = (lax.broadcasted_iota(jnp.int32, (rows, 1), 0) + pb * rows).astype(F32)
    row_real = (row_index < real_count).astype(F32)
    state = tokens_ref[...].astype(F32)
    lane = lax.broadcasted_iota(jnp.int32, (rows, 2 * width), 1)
    scale = 1.0 / HD**0.5

    def bias_wait(n, carry):
        for k in range(1, head_count):
            bias_copy(n, k).wait_recv()
        return carry

    for layer in range(LAYERS):
        if layer:
            forward_kv(layer)
        finish_kv(layer)
        if not layer:
            lax.fori_loop(0, steps, bias_wait, 0)
        keys_values = kv_all[layer].reshape(pb_count * rows, 2 * width)
        queries = query_gate[...]
        spread_q = jnp.concatenate(
            [
                jnp.where((lane >= h * HD) & (lane < (h + 1) * HD), queries, jnp.zeros_like(queries))
                for h in range(local_heads)
            ],
            axis=0,
        )
        bias = jnp.concatenate(
            [
                bias_in[source, layer].reshape(local_heads * rows, cols)
                for source in range(head_count)
            ],
            axis=1,
        )
        scores = matmul_t(spread_q, keys_values) * scale + bias.astype(F32)
        scores = jnp.where(is_real, scores, -1e30)
        peak = jnp.max(scores, axis=1, keepdims=True)
        weights = jnp.exp(scores - peak)
        total = jnp.sum(weights, axis=1, keepdims=True)
        mixed = matmul(weights.astype(BF16), keys_values) / total
        attended = jnp.zeros((rows, 2 * width), F32)
        for h in range(local_heads):
            keep = (lane >= width + h * HD) & (lane < width + (h + 1) * HD)
            attended = attended + jnp.where(keep, mixed[h * rows : (h + 1) * rows], 0.0)
        gated = (attended * jax.nn.sigmoid(queries.astype(F32))).astype(BF16)
        gated_all[layer, head] = gated[:, width:]
        for k in range(1, head_count):
            gated_copy(layer, k).start()
        for k in range(1, head_count):
            out_forward(layer, k).wait_recv()
        for copy in weight_copies(layer)[4:]:
            copy.wait()
        for k in range(1, head_count):
            gated_copy(layer, k).wait_recv()
        gathered = jnp.concatenate([gated_all[layer, h] for h in range(head_count)], axis=1)
        update = matmul(gathered, out_w[layer].reshape(head_count * width, features))
        state = state + row_real * update
        if layer == LAYERS - 1:
            result_ref[...] = state.astype(BF16)
        else:
            for copy in weight_copies(layer + 1)[:4]:
                copy.wait()
            project(layer + 1, normalize(state).astype(BF16))

    def bias_sent(n, carry):
        for k in range(1, head_count):
            bias_copy(n, k).wait_send()
        return carry

    lax.fori_loop(0, steps, bias_sent, 0)
    for layer in range(LAYERS):
        for d in range(1, chips):
            kv_copy(layer, d).wait_send()
        for d in range(chips):
            kv_forward(layer, d).wait_send()
        for k in range(1, head_count):
            gated_copy(layer, k).wait_send()
            out_copy(layer, k).wait_send()
            out_forward(layer, k).wait_send()


def on_device(
    head_count, pb_count, pair, tokens, token_mask, w_gu, w_down, w_bias, w_q, w_k, w_v, w_gate, w_out
):
    rows, cols, channels = pair.shape
    width = w_q.shape[2]
    features = tokens.shape[1]
    local_heads = width // HD
    chips = pb_count // CORES
    steps = (rows // STEP_ROWS) * (cols // LANES)
    vmem = pl.BlockSpec(memory_space=pltpu.VMEM)
    anywhere = pl.BlockSpec(memory_space=pl.ANY)
    dma = pltpu.SemaphoreType.DMA
    bias_shape = (head_count, LAYERS, local_heads, rows, cols)
    return pl.pallas_call(
        functools.partial(step_kernel, head_count, pb_count),
        out_shape=jax.ShapeDtypeStruct((rows, features), BF16),
        in_specs=[anywhere] + [vmem] * 5 + [anywhere] * 5,
        out_specs=vmem,
        scratch_shapes=[
            pltpu.VMEM(pair.shape, BF16),
            pltpu.VMEM(w_gu.shape, BF16),
            pltpu.VMEM((LAYERS, 4 * width, features), BF16),
            pltpu.VMEM((LAYERS, head_count, CORES, width // CORES, features), BF16),
            pltpu.VMEM(bias_shape, BF16),
            pltpu.VMEM(bias_shape, BF16),
            pltpu.VMEM((LAYERS, pb_count, rows, 2 * width), BF16),
            pltpu.VMEM((rows, 2 * width), BF16),
            pltpu.VMEM((LAYERS, head_count, rows, width), BF16),
            dma((steps,)),
            dma((LAYERS, 4 + CORES)),
            dma((steps, head_count)),
            dma((steps, head_count)),
            dma((LAYERS, chips)),
            dma((LAYERS, chips)),
            dma((LAYERS, chips)),
            dma((LAYERS, chips)),
            dma((LAYERS, head_count)),
            dma((LAYERS, head_count)),
            dma((LAYERS, head_count)),
            dma((LAYERS, head_count)),
            dma((LAYERS, head_count)),
            dma((LAYERS, head_count)),
        ],
        compiler_params=pltpu.CompilerParams(
            collective_id=0, has_side_effects=True, vmem_limit_bytes=60 * 1024 * 1024
        ),
        name="diffusion_step",
    )(
        pair,
        tokens,
        token_mask.reshape(1, -1),
        w_gu,
        w_down,
        w_bias.T,
        jnp.swapaxes(w_q, 1, 2),
        jnp.swapaxes(w_k, 1, 2),
        jnp.swapaxes(w_v, 1, 2),
        jnp.swapaxes(w_gate, 1, 2),
        w_out,
    )


def solution(mesh):
    placed = (
        P("pb", "head", None),
        P("pb", None),
        P(),
        P(),
        P(),
        P(),
        P(None, None, "head"),
        P(None, None, "head"),
        P(None, None, "head"),
        P(None, None, "head"),
        P(None, "head", None),
    )
    return jax.shard_map(
        functools.partial(on_device, mesh.shape["head"], mesh.shape["pb"]),
        mesh=mesh,
        in_specs=placed,
        out_specs=P("pb", None),
        check_vma=False,
    )
```

```python
import functools

import jax
import jax.numpy as jnp
from jax import lax
from jax.experimental import pallas as pl
from jax.experimental.pallas import tpu as pltpu
from jax.sharding import PartitionSpec as P

TRANS = 2
LAYERS = 2
HD = 48
CORES = 2
STEP_ROWS = 16
LANES = 128
F32 = jnp.float32
BF16 = jnp.bfloat16


def normalize(values):
    inverse = 1.0 / values.shape[-1]
    center = values - jnp.sum(values, axis=-1, keepdims=True) * inverse
    spread = jnp.sum(center * center, axis=-1, keepdims=True) * inverse
    return center * lax.rsqrt(spread + 1e-05)


def normalize_wide(values):
    inverse = 1.0 / values.shape[-1]
    center = values - jnp.sum(values, axis=-1, keepdims=True) * inverse
    ones = jnp.full((values.shape[-1], values.shape[-1]), inverse, BF16)
    spread = matmul((center * center).astype(BF16), ones)
    return center * lax.rsqrt(spread + 1e-05)


def matmul(left, right):
    return jnp.dot(left, right, preferred_element_type=F32)


def matmul_t(left, right):
    return lax.dot_general(left, right, (((1,), (1,)), ((), ())), preferred_element_type=F32)


def step_kernel(
    head_count,
    pb_count,
    pair_hbm,
    tokens_ref,
    mask_ref,
    gu_ref,
    down_ref,
    bias_w_ref,
    q_hbm,
    k_hbm,
    v_hbm,
    gate_hbm,
    out_hbm,
    result_ref,
    pair_v,
    gu_v,
    wide_w,
    out_w,
    bias_out,
    bias_in,
    kv_all,
    query_gate,
    gated_all,
    pair_sem,
    weight_sem,
    bias_send,
    bias_recv,
    kv_send,
    kv_recv,
    fwd_send,
    fwd_recv,
    gated_send,
    gated_recv,
    out_send,
    out_recv,
    out_fwd_send,
    out_fwd_recv,
):
    rows, cols, channels = pair_hbm.shape
    width = q_hbm.shape[1]
    features = tokens_ref.shape[1]
    local_heads = width // HD
    heads_all = local_heads * head_count
    half_width = width // CORES
    chips = pb_count // CORES
    col_blocks = cols // LANES
    steps = (rows // STEP_ROWS) * col_blocks
    hidden = down_ref.shape[1]

    head = lax.axis_index("head")
    pb = lax.axis_index("pb")
    core = lax.rem(pb, CORES)
    chip = pb // CORES
    partner = chip * CORES + (1 - core)

    def head_peer(k):
        return lax.rem(head + k, head_count)

    def chip_peer(d):
        return lax.rem(chip + d, chips) * CORES + core

    def chip_source(d):
        return lax.rem(chip + chips - d, chips) * CORES + core

    def projection_copies(layer):
        return [
            pltpu.make_async_copy(
                source.at[layer],
                wide_w.at[layer, index * width : (index + 1) * width],
                weight_sem.at[layer, index],
            )
            for index, source in enumerate((k_hbm, v_hbm, q_hbm, gate_hbm))
        ]

    def own_out_copies(layer):
        return [
            pltpu.make_async_copy(
                out_hbm.at[layer, part * half_width : (part + 1) * half_width],
                out_w.at[layer, head, part],
                weight_sem.at[layer, 4 + part],
            )
            for part in range(CORES)
        ]

    def pair_copy(n):
        where = (
            pl.ds((n // col_blocks) * STEP_ROWS, STEP_ROWS),
            pl.ds(pl.multiple_of((n % col_blocks) * LANES, LANES), LANES),
        )
        return pltpu.make_async_copy(
            pair_hbm.at[where[0], where[1], :], pair_v.at[where[0], where[1], :], pair_sem.at[n]
        )

    pair_copy(0).start()
    for copy in projection_copies(0):
        copy.start()
    for n in range(1, steps):
        pair_copy(n).start()
    for layer in range(LAYERS):
        for copy in own_out_copies(layer) + (projection_copies(layer) if layer else []):
            copy.start()

    barrier = pltpu.get_barrier_semaphore()
    for k in range(1, head_count):
        pl.semaphore_signal(
            barrier, inc=1, device_id=(head_peer(k), pb), device_id_type=pl.DeviceIdType.MESH
        )
    for d in range(1, chips):
        pl.semaphore_signal(
            barrier, inc=1, device_id=(head, chip_peer(d)), device_id_type=pl.DeviceIdType.MESH
        )
    pl.semaphore_signal(
        barrier, inc=1, device_id=(head, partner), device_id_type=pl.DeviceIdType.MESH
    )

    def remote(source, target, send, recv, where):
        return pltpu.make_async_remote_copy(
            src_ref=source,
            dst_ref=target,
            send_sem=send,
            recv_sem=recv,
            device_id=where,
            device_id_type=pl.DeviceIdType.MESH,
        )

    def kv_copy(layer, d):
        block = kv_all.at[layer, pb]
        return remote(
            block, block, kv_send.at[layer, d], kv_recv.at[layer, d], (head, chip_peer(d))
        )

    def kv_forward(layer, d):
        block = kv_all.at[layer, chip_source(d)]
        return remote(block, block, fwd_send.at[layer, d], fwd_recv.at[layer, d], (head, partner))

    def out_copy(layer, k):
        return remote(
            out_hbm.at[layer, pl.ds(pl.multiple_of(core * half_width, half_width), half_width)],
            out_w.at[layer, head, core],
            out_send.at[layer, k],
            out_recv.at[layer, k],
            (head_peer(k), pb),
        )

    def out_forward(layer, k):
        block = out_w.at[layer, lax.rem(head + head_count - k, head_count), core]
        return remote(
            block, block, out_fwd_send.at[layer, k], out_fwd_recv.at[layer, k], (head, partner)
        )

    def forward_out(layer):
        for k in range(1, head_count):
            out_copy(layer, k).wait_recv()
            out_forward(layer, k).start()

    def gated_copy(layer, k):
        block = gated_all.at[layer, head]
        return remote(
            block, block, gated_send.at[layer, k], gated_recv.at[layer, k], (head_peer(k), pb)
        )

    def project(layer, normed):
        kv_all[layer, pb] = matmul_t(normed, wide_w[layer, : 2 * width]).astype(BF16)
        if not layer:
            pl.semaphore_wait(barrier, head_count + chips - 1)
        for d in range(1, chips):
            kv_copy(layer, d).start()
        kv_forward(layer, 0).start()
        if not layer:
            for k in range(1, head_count):
                out_copy(0, k).start()
        query_gate[...] = matmul_t(normed, wide_w[layer, 2 * width :]).astype(BF16)

    def forward_kv(layer):
        for d in range(1, chips):
            kv_copy(layer, d).wait_recv()
            kv_forward(layer, d).start()

    def finish_kv(layer):
        for d in range(chips):
            kv_forward(layer, d).wait_recv()

    for section in range(TRANS):
        gu_v[section, :, :hidden] = (gu_ref[section, :, :hidden].astype(F32) * 0.5).astype(BF16)
        gu_v[section, :, hidden:] = gu_ref[section, :, hidden:]
    bias_w = bias_w_ref[...]

    def bias_copy(n, layer, k):
        where = (
            pl.ds((n // col_blocks) * STEP_ROWS, STEP_ROWS),
            pl.ds(pl.multiple_of((n % col_blocks) * LANES, LANES), LANES),
        )
        return remote(
            bias_out.at[head_peer(k), layer, :, where[0], where[1]],
            bias_in.at[head, layer, :, where[0], where[1]],
            bias_send.at[n, layer, k],
            bias_recv.at[n, layer, k],
            (head_peer(k), pb),
        )

    half = STEP_ROWS // 2

    def pair_step(n, carry):
        pair_copy(n).wait()
        first_row = (n // col_blocks) * STEP_ROWS
        first_col = pl.multiple_of((n % col_blocks) * LANES, LANES)

        planes = []
        for part in range(2):
            current = pair_v[
                pl.ds(first_row + part * half, half), pl.ds(first_col, LANES), :
            ].reshape(half * LANES, channels)
            for section in range(TRANS):
                wide = current.astype(F32)
                normed = normalize_wide(wide).astype(BF16)
                mixed = matmul(normed, gu_v[section])
                gate = mixed[:, :hidden]
                units = ((gate + gate * jnp.tanh(gate)) * mixed[:, hidden:]).astype(BF16)
                current = (wide + matmul(units, down_ref[section])).astype(BF16)
            normed = normalize_wide(current.astype(F32)).astype(BF16)
            projected = matmul_t(bias_w, normed)
            planes += [projected[:, i * LANES : (i + 1) * LANES] for i in range(half)]
        by_head = jnp.transpose(jnp.stack(planes, axis=0), (1, 0, 2)).astype(BF16)
        for layer in range(LAYERS):
            for target in range(head_count):
                start = layer * heads_all + target * local_heads
                bias_out[target, layer, :, pl.ds(first_row, STEP_ROWS), pl.ds(first_col, LANES)] = (
                    by_head[start : start + local_heads]
                )
        bias_in[head, :, :, pl.ds(first_row, STEP_ROWS), pl.ds(first_col, LANES)] = bias_out[
            head, :, :, pl.ds(first_row, STEP_ROWS), pl.ds(first_col, LANES)
        ]

        @pl.when(n == 0)
        def _():
            for copy in projection_copies(0):
                copy.wait()
            project(0, normalize(tokens_ref[...].astype(F32)).astype(BF16))

        for layer in range(LAYERS):
            for k in range(1, head_count):
                bias_copy(n, layer, k).start()

        @pl.when(n == steps - 2)
        def _():
            forward_kv(0)
            forward_out(0)

        return carry

    lax.fori_loop(0, steps, pair_step, 0)

    mask_row = mask_ref[...]
    real_count = jnp.sum(mask_row.astype(F32), axis=1, keepdims=True)
    is_real = mask_row == 1
    row_index = (lax.broadcasted_iota(jnp.int32, (rows, 1), 0) + pb * rows).astype(F32)
    row_real = (row_index < real_count).astype(F32)
    state = tokens_ref[...].astype(F32)
    lane = lax.broadcasted_iota(jnp.int32, (rows, 2 * width), 1)
    scale = 1.0 / HD**0.5

    def bias_wait(layer, n, carry):
        for k in range(1, head_count):
            bias_copy(n, layer, k).wait_recv()
        return carry

    for layer in range(LAYERS):
        if layer:
            forward_kv(layer)
        finish_kv(layer)
        keys_values = kv_all[layer].reshape(pb_count * rows, 2 * width)
        queries = query_gate[...]
        spread_q = jnp.concatenate(
            [
                jnp.where((lane >= h * HD) & (lane < (h + 1) * HD), queries, jnp.zeros_like(queries))
                for h in range(local_heads)
            ],
            axis=0,
        )
        scores = matmul_t(spread_q, keys_values) * scale
        lax.fori_loop(0, steps, functools.partial(bias_wait, layer), 0)
        bias = jnp.concatenate(
            [
                bias_in[source, layer].reshape(local_heads * rows, cols)
                for source in range(head_count)
            ],
            axis=1,
        )
        scores = scores + bias.astype(F32)
        scores = jnp.where(is_real, scores, -1e30)
        peak = jnp.max(scores, axis=1, keepdims=True)
        weights = jnp.exp(scores - peak)
        total = jnp.sum(weights, axis=1, keepdims=True)
        mixed = matmul(weights.astype(BF16), keys_values) / total
        attended = jnp.zeros((rows, 2 * width), F32)
        for h in range(local_heads):
            keep = (lane >= width + h * HD) & (lane < width + (h + 1) * HD)
            attended = attended + jnp.where(keep, mixed[h * rows : (h + 1) * rows], 0.0)
        gated = (attended * jax.nn.sigmoid(queries.astype(F32))).astype(BF16)
        gated_all[layer, head] = gated[:, width:]
        for k in range(1, head_count):
            gated_copy(layer, k).start()
        if layer:
            forward_out(layer)
        for k in range(1, head_count):
            out_forward(layer, k).wait_recv()
        for copy in own_out_copies(layer):
            copy.wait()
        for k in range(1, head_count):
            gated_copy(layer, k).wait_recv()
        if layer + 1 < LAYERS:
            for k in range(1, head_count):
                out_copy(layer + 1, k).start()
        gathered = jnp.concatenate([gated_all[layer, h] for h in range(head_count)], axis=1)
        update = matmul(gathered, out_w[layer].reshape(head_count * width, features))
        state = state + row_real * update
        if layer == LAYERS - 1:
            result_ref[...] = state.astype(BF16)
        else:
            for copy in projection_copies(layer + 1):
                copy.wait()
            project(layer + 1, normalize(state).astype(BF16))

    def bias_sent(n, carry):
        for layer in range(LAYERS):
            for k in range(1, head_count):
                bias_copy(n, layer, k).wait_send()
        return carry

    lax.fori_loop(0, steps, bias_sent, 0)
    for layer in range(LAYERS):
        for d in range(1, chips):
            kv_copy(layer, d).wait_send()
        for d in range(chips):
            kv_forward(layer, d).wait_send()
        for k in range(1, head_count):
            gated_copy(layer, k).wait_send()
            out_copy(layer, k).wait_send()
            out_forward(layer, k).wait_send()


def on_device(
    head_count, pb_count, pair, tokens, token_mask, w_gu, w_down, w_bias, w_q, w_k, w_v, w_gate, w_out
):
    rows, cols, channels = pair.shape
    width = w_q.shape[2]
    features = tokens.shape[1]
    local_heads = width // HD
    chips = pb_count // CORES
    steps = (rows // STEP_ROWS) * (cols // LANES)
    vmem = pl.BlockSpec(memory_space=pltpu.VMEM)
    anywhere = pl.BlockSpec(memory_space=pl.ANY)
    dma = pltpu.SemaphoreType.DMA
    bias_shape = (head_count, LAYERS, local_heads, rows, cols)
    return pl.pallas_call(
        functools.partial(step_kernel, head_count, pb_count),
        out_shape=jax.ShapeDtypeStruct((rows, features), BF16),
        in_specs=[anywhere] + [vmem] * 5 + [anywhere] * 5,
        out_specs=vmem,
        scratch_shapes=[
            pltpu.VMEM(pair.shape, BF16),
            pltpu.VMEM(w_gu.shape, BF16),
            pltpu.VMEM((LAYERS, 4 * width, features), BF16),
            pltpu.VMEM((LAYERS, head_count, CORES, width // CORES, features), BF16),
            pltpu.VMEM(bias_shape, BF16),
            pltpu.VMEM(bias_shape, BF16),
            pltpu.VMEM((LAYERS, pb_count, rows, 2 * width), BF16),
            pltpu.VMEM((rows, 2 * width), BF16),
            pltpu.VMEM((LAYERS, head_count, rows, width), BF16),
            dma((steps,)),
            dma((LAYERS, 4 + CORES)),
            dma((steps, LAYERS, head_count)),
            dma((steps, LAYERS, head_count)),
            dma((LAYERS, chips)),
            dma((LAYERS, chips)),
            dma((LAYERS, chips)),
            dma((LAYERS, chips)),
            dma((LAYERS, head_count)),
            dma((LAYERS, head_count)),
            dma((LAYERS, head_count)),
            dma((LAYERS, head_count)),
            dma((LAYERS, head_count)),
            dma((LAYERS, head_count)),
        ],
        compiler_params=pltpu.CompilerParams(
            collective_id=0, has_side_effects=True, vmem_limit_bytes=60 * 1024 * 1024
        ),
        name="diffusion_step",
    )(
        pair,
        tokens,
        token_mask.reshape(1, -1),
        w_gu,
        w_down,
        w_bias.T,
        jnp.swapaxes(w_q, 1, 2),
        jnp.swapaxes(w_k, 1, 2),
        jnp.swapaxes(w_v, 1, 2),
        jnp.swapaxes(w_gate, 1, 2),
        w_out,
    )


def solution(mesh):
    placed = (
        P("pb", "head", None),
        P("pb", None),
        P(),
        P(),
        P(),
        P(),
        P(None, None, "head"),
        P(None, None, "head"),
        P(None, None, "head"),
        P(None, None, "head"),
        P(None, "head", None),
    )
    return jax.shard_map(
        functools.partial(on_device, mesh.shape["head"], mesh.shape["pb"]),
        mesh=mesh,
        in_specs=placed,
        out_specs=P("pb", None),
        check_vma=False,
    )
```

```python
import functools

import jax
import jax.numpy as jnp
from jax import lax
from jax.experimental import pallas as pl
from jax.experimental.pallas import tpu as pltpu
from jax.sharding import PartitionSpec as P

TRANS = 2
LAYERS = 2
HD = 48
CORES = 2
STEP_ROWS = 16
LANES = 128
F32 = jnp.float32
BF16 = jnp.bfloat16


def normalize(values):
    inverse = 1.0 / values.shape[-1]
    center = values - jnp.sum(values, axis=-1, keepdims=True) * inverse
    spread = jnp.sum(center * center, axis=-1, keepdims=True) * inverse
    return center * lax.rsqrt(spread + 1e-05)


def normalize_wide(values):
    inverse = 1.0 / values.shape[-1]
    center = values - jnp.sum(values, axis=-1, keepdims=True) * inverse
    ones = jnp.full((values.shape[-1], values.shape[-1]), inverse, BF16)
    spread = matmul((center * center).astype(BF16), ones)
    return center * lax.rsqrt(spread + 1e-05)


def matmul(left, right):
    return jnp.dot(left, right, preferred_element_type=F32)


def matmul_t(left, right):
    return lax.dot_general(left, right, (((1,), (1,)), ((), ())), preferred_element_type=F32)


def step_kernel(
    head_count,
    pb_count,
    pair_hbm,
    tokens_hbm,
    mask_ref,
    gu_hbm,
    down_hbm,
    bias_w_hbm,
    q_hbm,
    k_hbm,
    v_hbm,
    gate_hbm,
    out_hbm,
    result_ref,
    tokens_ref,
    gu_ref,
    down_ref,
    bias_w_ref,
    pair_v,
    gu_v,
    wide_w,
    out_w,
    bias_out,
    bias_in,
    kv_all,
    query_gate,
    gated_all,
    pair_sem,
    weight_sem,
    small_sem,
    bias_send,
    bias_recv,
    kv_send,
    kv_recv,
    fwd_send,
    fwd_recv,
    gated_send,
    gated_recv,
    out_send,
    out_recv,
    out_fwd_send,
    out_fwd_recv,
):
    rows, cols, channels = pair_hbm.shape
    width = q_hbm.shape[1]
    features = tokens_ref.shape[1]
    local_heads = width // HD
    heads_all = local_heads * head_count
    half_width = width // CORES
    chips = pb_count // CORES
    col_blocks = cols // LANES
    steps = (rows // STEP_ROWS) * col_blocks
    hidden = down_ref.shape[1]

    head = lax.axis_index("head")
    pb = lax.axis_index("pb")
    core = lax.rem(pb, CORES)
    chip = pb // CORES
    partner = chip * CORES + (1 - core)

    def head_peer(k):
        return lax.rem(head + k, head_count)

    def chip_peer(d):
        return lax.rem(chip + d, chips) * CORES + core

    def chip_source(d):
        return lax.rem(chip + chips - d, chips) * CORES + core

    barrier = pltpu.get_barrier_semaphore()
    for k in range(1, head_count):
        pl.semaphore_signal(
            barrier, inc=1, device_id=(head_peer(k), pb), device_id_type=pl.DeviceIdType.MESH
        )
    for d in range(1, chips):
        pl.semaphore_signal(
            barrier, inc=1, device_id=(head, chip_peer(d)), device_id_type=pl.DeviceIdType.MESH
        )
    pl.semaphore_signal(
        barrier, inc=1, device_id=(head, partner), device_id_type=pl.DeviceIdType.MESH
    )

    def projection_copies(layer):
        return [
            pltpu.make_async_copy(
                source.at[layer],
                wide_w.at[layer, index * width : (index + 1) * width],
                weight_sem.at[layer, index],
            )
            for index, source in enumerate((k_hbm, v_hbm, q_hbm, gate_hbm))
        ]

    def own_out_copies(layer):
        return [
            pltpu.make_async_copy(
                out_hbm.at[layer, part * half_width : (part + 1) * half_width],
                out_w.at[layer, head, part],
                weight_sem.at[layer, 4 + part],
            )
            for part in range(CORES)
        ]

    def pair_copy(n):
        where = (
            pl.ds((n // col_blocks) * STEP_ROWS, STEP_ROWS),
            pl.ds(pl.multiple_of((n % col_blocks) * LANES, LANES), LANES),
        )
        return pltpu.make_async_copy(
            pair_hbm.at[where[0], where[1], :], pair_v.at[where[0], where[1], :], pair_sem.at[n]
        )

    small_copies = [
        pltpu.make_async_copy(source, target, small_sem.at[index])
        for index, (source, target) in enumerate(
            (
                (gu_hbm, gu_ref),
                (down_hbm, down_ref),
                (bias_w_hbm, bias_w_ref),
                (tokens_hbm, tokens_ref),
            )
        )
    ]
    small_copies[0].start()
    pair_copy(0).start()
    for copy in small_copies[1:] + projection_copies(0):
        copy.start()
    for n in range(1, steps):
        pair_copy(n).start()
    for layer in range(LAYERS):
        for copy in own_out_copies(layer) + (projection_copies(layer) if layer else []):
            copy.start()

    def remote(source, target, send, recv, where):
        return pltpu.make_async_remote_copy(
            src_ref=source,
            dst_ref=target,
            send_sem=send,
            recv_sem=recv,
            device_id=where,
            device_id_type=pl.DeviceIdType.MESH,
        )

    def kv_copy(layer, d):
        block = kv_all.at[layer, pb]
        return remote(
            block, block, kv_send.at[layer, d], kv_recv.at[layer, d], (head, chip_peer(d))
        )

    def kv_forward(layer, d):
        block = kv_all.at[layer, chip_source(d)]
        return remote(block, block, fwd_send.at[layer, d], fwd_recv.at[layer, d], (head, partner))

    def out_copy(layer, k):
        return remote(
            out_hbm.at[layer, pl.ds(pl.multiple_of(core * half_width, half_width), half_width)],
            out_w.at[layer, head, core],
            out_send.at[layer, k],
            out_recv.at[layer, k],
            (head_peer(k), pb),
        )

    def out_forward(layer, k):
        block = out_w.at[layer, lax.rem(head + head_count - k, head_count), core]
        return remote(
            block, block, out_fwd_send.at[layer, k], out_fwd_recv.at[layer, k], (head, partner)
        )

    def forward_out(layer):
        for k in range(1, head_count):
            out_copy(layer, k).wait_recv()
            out_forward(layer, k).start()

    def gated_copy(layer, k):
        block = gated_all.at[layer, head]
        return remote(
            block, block, gated_send.at[layer, k], gated_recv.at[layer, k], (head_peer(k), pb)
        )

    def project(layer, normed):
        kv_all[layer, pb] = matmul_t(normed, wide_w[layer, : 2 * width]).astype(BF16)
        if not layer:
            pl.semaphore_wait(barrier, head_count + chips - 1)
        for d in range(1, chips):
            kv_copy(layer, d).start()
        kv_forward(layer, 0).start()
        if not layer:
            for k in range(1, head_count):
                out_copy(0, k).start()
        query_gate[...] = matmul_t(normed, wide_w[layer, 2 * width :]).astype(BF16)

    def forward_kv(layer):
        for d in range(1, chips):
            kv_copy(layer, d).wait_recv()
            kv_forward(layer, d).start()

    def finish_kv(layer):
        for d in range(chips):
            kv_forward(layer, d).wait_recv()

    for copy in small_copies:
        copy.wait()

    for section in range(TRANS):
        gu_v[section, :, :hidden] = (gu_ref[section, :, :hidden].astype(F32) * 0.5).astype(BF16)
        gu_v[section, :, hidden:] = gu_ref[section, :, hidden:]
    bias_w = bias_w_ref[...]

    def bias_copy(n, layer, k):
        where = (
            pl.ds((n // col_blocks) * STEP_ROWS, STEP_ROWS),
            pl.ds(pl.multiple_of((n % col_blocks) * LANES, LANES), LANES),
        )
        return remote(
            bias_out.at[head_peer(k), layer, :, where[0], where[1]],
            bias_in.at[head, layer, :, where[0], where[1]],
            bias_send.at[n, layer, k],
            bias_recv.at[n, layer, k],
            (head_peer(k), pb),
        )

    half = STEP_ROWS // 2

    def pair_step(n, carry):
        pair_copy(n).wait()
        first_row = (n // col_blocks) * STEP_ROWS
        first_col = pl.multiple_of((n % col_blocks) * LANES, LANES)

        planes = []
        for part in range(2):
            current = pair_v[
                pl.ds(first_row + part * half, half), pl.ds(first_col, LANES), :
            ].reshape(half * LANES, channels)
            for section in range(TRANS):
                wide = current.astype(F32)
                normed = normalize_wide(wide).astype(BF16)
                mixed = matmul(normed, gu_v[section])
                gate = mixed[:, :hidden]
                units = ((gate + gate * jnp.tanh(gate)) * mixed[:, hidden:]).astype(BF16)
                current = (wide + matmul(units, down_ref[section])).astype(BF16)
            normed = normalize_wide(current.astype(F32)).astype(BF16)
            projected = matmul_t(bias_w, normed)
            planes += [projected[:, i * LANES : (i + 1) * LANES] for i in range(half)]
        by_head = jnp.transpose(jnp.stack(planes, axis=0), (1, 0, 2)).astype(BF16)
        for layer in range(LAYERS):
            for target in range(head_count):
                start = layer * heads_all + target * local_heads
                bias_out[target, layer, :, pl.ds(first_row, STEP_ROWS), pl.ds(first_col, LANES)] = (
                    by_head[start : start + local_heads]
                )
        bias_in[head, :, :, pl.ds(first_row, STEP_ROWS), pl.ds(first_col, LANES)] = bias_out[
            head, :, :, pl.ds(first_row, STEP_ROWS), pl.ds(first_col, LANES)
        ]

        @pl.when(n == 0)
        def _():
            for copy in projection_copies(0):
                copy.wait()
            project(0, normalize(tokens_ref[...].astype(F32)).astype(BF16))

        for layer in range(LAYERS):
            for k in range(1, head_count):
                bias_copy(n, layer, k).start()

        @pl.when(n == steps - 2)
        def _():
            forward_kv(0)
            forward_out(0)

        return carry

    lax.fori_loop(0, steps, pair_step, 0)

    mask_row = mask_ref[...]
    real_count = jnp.sum(mask_row.astype(F32), axis=1, keepdims=True)
    is_real = mask_row == 1
    row_index = (lax.broadcasted_iota(jnp.int32, (rows, 1), 0) + pb * rows).astype(F32)
    row_real = (row_index < real_count).astype(F32)
    state = tokens_ref[...].astype(F32)
    lane = lax.broadcasted_iota(jnp.int32, (rows, 2 * width), 1)
    scale = 1.0 / HD**0.5

    def bias_wait(layer, n, carry):
        for k in range(1, head_count):
            bias_copy(n, layer, k).wait_recv()
        return carry

    for layer in range(LAYERS):
        if layer:
            forward_kv(layer)
        finish_kv(layer)
        keys_values = kv_all[layer].reshape(pb_count * rows, 2 * width)
        queries = query_gate[...]
        spread_q = jnp.concatenate(
            [
                jnp.where((lane >= h * HD) & (lane < (h + 1) * HD), queries, jnp.zeros_like(queries))
                for h in range(local_heads)
            ],
            axis=0,
        )
        scores = matmul_t(spread_q, keys_values) * scale
        lax.fori_loop(0, steps, functools.partial(bias_wait, layer), 0)
        bias = jnp.concatenate(
            [
                bias_in[source, layer].reshape(local_heads * rows, cols)
                for source in range(head_count)
            ],
            axis=1,
        )
        scores = scores + bias.astype(F32)
        scores = jnp.where(is_real, scores, -1e30)
        peak = jnp.max(scores, axis=1, keepdims=True)
        weights = jnp.exp(scores - peak)
        total = jnp.sum(weights, axis=1, keepdims=True)
        mixed = matmul(weights.astype(BF16), keys_values) / total
        attended = jnp.zeros((rows, 2 * width), F32)
        for h in range(local_heads):
            keep = (lane >= width + h * HD) & (lane < width + (h + 1) * HD)
            attended = attended + jnp.where(keep, mixed[h * rows : (h + 1) * rows], 0.0)
        gated = (attended * jax.nn.sigmoid(queries.astype(F32))).astype(BF16)
        gated_all[layer, head] = gated[:, width:]
        for k in range(1, head_count):
            gated_copy(layer, k).start()
        if layer:
            forward_out(layer)
        for k in range(1, head_count):
            out_forward(layer, k).wait_recv()
        for copy in own_out_copies(layer):
            copy.wait()
        for k in range(1, head_count):
            gated_copy(layer, k).wait_recv()
        if layer + 1 < LAYERS:
            for k in range(1, head_count):
                out_copy(layer + 1, k).start()
        gathered = jnp.concatenate([gated_all[layer, h] for h in range(head_count)], axis=1)
        update = matmul(gathered, out_w[layer].reshape(head_count * width, features))
        state = state + row_real * update
        if layer == LAYERS - 1:
            result_ref[...] = state.astype(BF16)
        else:
            for copy in projection_copies(layer + 1):
                copy.wait()
            project(layer + 1, normalize(state).astype(BF16))

    def bias_sent(n, carry):
        for layer in range(LAYERS):
            for k in range(1, head_count):
                bias_copy(n, layer, k).wait_send()
        return carry

    lax.fori_loop(0, steps, bias_sent, 0)
    for layer in range(LAYERS):
        for d in range(1, chips):
            kv_copy(layer, d).wait_send()
        for d in range(chips):
            kv_forward(layer, d).wait_send()
        for k in range(1, head_count):
            gated_copy(layer, k).wait_send()
            out_copy(layer, k).wait_send()
            out_forward(layer, k).wait_send()


def on_device(
    head_count, pb_count, pair, tokens, token_mask, w_gu, w_down, w_bias, w_q, w_k, w_v, w_gate, w_out
):
    rows, cols, channels = pair.shape
    width = w_q.shape[2]
    features = tokens.shape[1]
    local_heads = width // HD
    chips = pb_count // CORES
    steps = (rows // STEP_ROWS) * (cols // LANES)
    vmem = pl.BlockSpec(memory_space=pltpu.VMEM)
    anywhere = pl.BlockSpec(memory_space=pl.ANY)
    dma = pltpu.SemaphoreType.DMA
    bias_shape = (head_count, LAYERS, local_heads, rows, cols)
    return pl.pallas_call(
        functools.partial(step_kernel, head_count, pb_count),
        out_shape=jax.ShapeDtypeStruct((rows, features), BF16),
        in_specs=[anywhere, anywhere, vmem] + [anywhere] * 8,
        out_specs=vmem,
        scratch_shapes=[
            pltpu.VMEM(tokens.shape, BF16),
            pltpu.VMEM(w_gu.shape, BF16),
            pltpu.VMEM(w_down.shape, BF16),
            pltpu.VMEM(w_bias.shape[::-1], BF16),
            pltpu.VMEM(pair.shape, BF16),
            pltpu.VMEM(w_gu.shape, BF16),
            pltpu.VMEM((LAYERS, 4 * width, features), BF16),
            pltpu.VMEM((LAYERS, head_count, CORES, width // CORES, features), BF16),
            pltpu.VMEM(bias_shape, BF16),
            pltpu.VMEM(bias_shape, BF16),
            pltpu.VMEM((LAYERS, pb_count, rows, 2 * width), BF16),
            pltpu.VMEM((rows, 2 * width), BF16),
            pltpu.VMEM((LAYERS, head_count, rows, width), BF16),
            dma((steps,)),
            dma((LAYERS, 4 + CORES)),
            dma((4,)),
            dma((steps, LAYERS, head_count)),
            dma((steps, LAYERS, head_count)),
            dma((LAYERS, chips)),
            dma((LAYERS, chips)),
            dma((LAYERS, chips)),
            dma((LAYERS, chips)),
            dma((LAYERS, head_count)),
            dma((LAYERS, head_count)),
            dma((LAYERS, head_count)),
            dma((LAYERS, head_count)),
            dma((LAYERS, head_count)),
            dma((LAYERS, head_count)),
        ],
        compiler_params=pltpu.CompilerParams(
            collective_id=0, has_side_effects=True, vmem_limit_bytes=60 * 1024 * 1024
        ),
        name="diffusion_step",
    )(
        pair,
        tokens,
        token_mask.reshape(1, -1),
        w_gu,
        w_down,
        w_bias.T,
        jnp.swapaxes(w_q, 1, 2),
        jnp.swapaxes(w_k, 1, 2),
        jnp.swapaxes(w_v, 1, 2),
        jnp.swapaxes(w_gate, 1, 2),
        w_out,
    )


def solution(mesh):
    placed = (
        P("pb", "head", None),
        P("pb", None),
        P(),
        P(),
        P(),
        P(),
        P(None, None, "head"),
        P(None, None, "head"),
        P(None, None, "head"),
        P(None, None, "head"),
        P(None, "head", None),
    )
    return jax.shard_map(
        functools.partial(on_device, mesh.shape["head"], mesh.shape["pb"]),
        mesh=mesh,
        in_specs=placed,
        out_specs=P("pb", None),
        check_vma=False,
    )
```
